32 devices in a mesh: col: 16 (over z, y, x), row: 2 (over core).
Axes of the slice: x: 2, y: 2, z: 4, core: 2. Of those that a mesh axis runs over, the one named last changes fastest.
Arguments:
- top_rows: float32 [1792, 8192], P(None, ('col', 'row')), may hold values from -0.0625 to 0.0625
- lower_new: float32 [8192, 256], P(('col', 'row')), may hold values from -6 to 6
- block_order: int32 [32, 2], P(('col', 'row')), may hold values from 0 to 1, each once within a row
- corner: float32 [1792, 1792], P('row'), may hold values from -0.125 to 0.125
- target: float32 [1792, 256], P('row'), may hold values from -6 to 6
- coupling: float32 [128, 128], replicated, may hold values from -0.5 to 0.5
- top_right: float32 [14, 128, 128], P('row'), may hold values from -0.5 to 0.5
- top_left: float32 [14, 128, 128], P('row'), may hold values from -0.5 to 0.5
- top_values: float32 [14, 128], P('row'), may hold values from 0.5 to 2
- new_right: float32 [2, 128, 128], replicated, may hold values from -0.5 to 0.5
- new_left: float32 [2, 128, 128], replicated, may hold values from -0.5 to 0.5
- new_values: float32 [2, 128], replicated, may hold values from 0.5 to 2
Outputs:
- solution: float32 [1792, 256], P('row')
The draws below stay inside these ranges and needn't reach their ends.
Inputs may be any that keep to these rules, and one draw needn't show every extreme that they name: Each row of block_order is an ordering of 0 to 1.
All inputs are finite; a program needn't handle non-finite values.
Results may differ from the reference program's by a relative error of at most 0.0001.
Values sent between devices are 32-bit elements; how exact they have to be, the bound alone decides.
No kernel may reach another device: no remote copies, remote signals or barrier semaphores. Data moves between devices by JAX's collectives and lax.ppermute only.
A program may use at most 64 MiB of HBM per device.

```python
import math
import jax
import jax.numpy as jnp
from jax import lax

B = 128
R = 14
KB_DEV = 2
K = 64


def levels(rng, dims, split, low, high):
    def one(axis_at, parts):
        heights = jax.random.uniform(jax.random.fold_in(jax.random.fold_in(rng, 6), axis_at), (parts,), jnp.float32, low / len(split), high / len(split))
        return jnp.repeat(jnp.exp(heights), dims[axis_at] // parts).reshape((-1,) + (1,) * (len(dims) - axis_at - 1))

    level = one(*split[0])
    for cut in split[1:]:
        level = level * one(*cut)
    return level


def centred(own_key, dims, deviation, most, cuts=(), held_as=jnp.bfloat16):
    level = levels(own_key, dims, cuts, -0.22, 0.18) if cuts else 1.0
    array = jax.random.normal(own_key, dims, jnp.float32) * deviation * level
    return jnp.minimum(jnp.maximum(array, -most), most).astype(held_as)


def setup_inputs(seed: int = 0) -> dict:
    keys = jax.random.split(jax.random.key(seed), 13)
    top_rows = centred(keys[0], (R * B, K * B), (K * B) ** -0.5, 0.0625, ((1, 32),), jnp.float32)
    lower_new = centred(keys[1], (K * B, 2 * B), 1.0, 6.0, ((0, 32),), jnp.float32)
    block_order = jax.vmap(lambda own: jax.random.permutation(own, KB_DEV))(jax.random.split(keys[2], (K // KB_DEV))).reshape((K // KB_DEV, KB_DEV)).astype(jnp.int32)
    corner = centred(keys[3], (R * B, R * B), (R * B) ** -0.5, 0.125, ((0, 2),), jnp.float32)
    target = centred(keys[4], (R * B, 2 * B), 1.0, 6.0, ((0, 2),), jnp.float32)
    coupling = centred(keys[5], (B, B), B ** -0.5, 0.5, (), jnp.float32)
    top_right = centred(keys[6], (R, B, B), B ** -0.5, 0.5, ((0, 2),), jnp.float32)
    top_left = centred(keys[7], (R, B, B), B ** -0.5, 0.5, ((0, 2),), jnp.float32)
    top_values = jnp.clip(jnp.exp(math.log(2.0) - 1.3862944 * jax.random.uniform(keys[8], (R, B), jnp.float32) ** levels(keys[8], (R, B), ((0, 2),), -0.2, 0.2)), 0.5, 2.0)
    new_right = centred(keys[9], (2, B, B), B ** -0.5, 0.5, (), jnp.float32)
    new_left = centred(keys[10], (2, B, B), B ** -0.5, 0.5, (), jnp.float32)
    new_values = jnp.clip(jnp.exp(jax.random.uniform(keys[11], (2, B), jnp.float32, math.log(0.5), math.log(2.0))), 0.5, 2.0)
    return {"top_rows": top_rows, "lower_new": lower_new, "block_order": block_order, "corner": corner, "target": target, "coupling": coupling, "top_right": top_right, "top_left": top_left, "top_values": top_values, "new_right": new_right, "new_left": new_left, "new_values": new_values}


PRECISION = lax.Precision.HIGHEST


def solve_block(right_side, left_right, left_left, left_values, col_right, col_left, col_values):
    rotated = jnp.dot(jnp.dot(left_left, right_side, precision=PRECISION), col_right, precision=PRECISION)
    rotated = rotated / (left_values[:, None] + col_values[None, :])
    return jnp.dot(jnp.dot(left_right, rotated, precision=PRECISION), col_left, precision=PRECISION)


def reference(top_rows, lower_new, block_order, corner, target, coupling, top_right, top_left, top_values, new_right, new_left, new_values):
    groups = K // KB_DEV
    lower_blocks = lower_new.reshape(groups, KB_DEV, B, 2 * B)
    paired = jnp.take_along_axis(lower_blocks, block_order[:, :, None, None].astype(jnp.int32), axis=1).reshape(K * B, 2 * B)
    right_side = target - jnp.dot(top_rows, paired, precision=PRECISION)
    row_block = jnp.arange(R * B) // B
    upper_part = jnp.where(row_block[:, None] < row_block[None, :], corner, jnp.zeros_like(corner))
    solved = [None] * R
    for position in range(R - 1, -1, -1):
        offset = position * B
        left_column = solve_block(right_side[offset:offset + B, :B], top_right[position], top_left[position], top_values[position], new_right[0], new_left[0], new_values[0])
        second_side = right_side[offset:offset + B, B:] - jnp.dot(left_column, coupling, precision=PRECISION)
        right_column = solve_block(second_side, top_right[position], top_left[position], top_values[position], new_right[1], new_left[1], new_values[1])
        combined = jnp.concatenate([left_column, right_column], axis=1)
        right_side = right_side - jnp.dot(upper_part[:, offset:offset + B], combined, precision=PRECISION)
        solved[position] = combined
    return jnp.concatenate(solved, axis=0)
```

```python
import functools

import jax
import jax.numpy as jnp
from jax import lax
from jax.experimental import pallas as pl
from jax.experimental.pallas import tpu as pltpu
from jax.sharding import PartitionSpec as P

F32 = jnp.float32
BF16 = jnp.bfloat16

VMEM = pl.BlockSpec(memory_space=pltpu.VMEM)
SMEM = pl.BlockSpec(memory_space=pltpu.SMEM)


def split(x):
    high = x.astype(BF16)
    return high, (x - high.astype(F32)).astype(BF16)


def mm(a, b):
    return jnp.dot(a, b, preferred_element_type=F32)


def dot_parts(a, b):
    (ah, al), (bh, bl) = a, b
    return mm(ah, bh) + (mm(ah, bl) + mm(al, bh))


def dot3(a, b):
    return dot_parts(split(a), split(b))


def partial_kernel(where, order, a_ref, b_ref, out_ref):
    slots, depth, _ = out_ref.shape
    size = b_ref.shape[0] // order.shape[1]
    paired = [
        b_ref[pl.ds(pl.multiple_of(order[0, g] * size, size), size), :]
        for g in range(order.shape[1])
    ]
    paired = split(jnp.concatenate(paired, axis=0))
    for m in range(slots):
        rows = pl.multiple_of((where[0] ^ m) * depth, 8)
        out_ref[m] = dot_parts(split(a_ref[pl.ds(rows, depth), :]), paired)


def partial_product(where, half, order, top_rows, lower, slots):
    rows = top_rows.shape[0] // 2
    width = lower.shape[1]
    return pl.pallas_call(
        lambda half_ref, *refs: partial_kernel(*refs),
        out_shape=jax.ShapeDtypeStruct((slots, rows // slots, width), F32),
        grid_spec=pltpu.PrefetchScalarGridSpec(
            num_scalar_prefetch=1,
            grid=(1,),
            in_specs=[
                SMEM,
                SMEM,
                pl.BlockSpec((rows, top_rows.shape[1]), lambda i, h: (h[0], 0)),
                pl.BlockSpec(lower.shape, lambda i, h: (0, 0)),
            ],
            out_specs=pl.BlockSpec((slots, rows // slots, width), lambda i, h: (0, 0, 0)),
        ),
        name="partial_product",
    )(half, where, order, top_rows, lower)


def prepare_kernel(
    row, own_ref, off_ref, q_ref, p_ref, po_ref, e_ref, nr_ref, nl_ref,
    diag_ref, toff_ref, s_ref, g_ref,
):
    i = pl.program_id(0)
    blocks, n, _ = p_ref.shape
    q = split(q_ref[0])
    s_ref[0] = dot_parts(q, split(p_ref[i]))
    own = dot_parts(q, split(own_ref[...]))
    off = dot_parts(q, split(off_ref[...]))
    for k in range(blocks):
        cols = slice(k * n, (k + 1) * n)
        toff_ref[:, cols] = dot3(off[:, cols], po_ref[k])
        diag_ref[:, cols] = dot3(own[:, cols], p_ref[k])

    @pl.when(i == 0)
    def _():
        g_ref[0] = dot3(nl_ref[0], nr_ref[0])
        g_ref[1] = dot3(dot3(nl_ref[0], e_ref[...]), nr_ref[1])
        g_ref[2] = dot3(nl_ref[1], nr_ref[1])


def prepare(row, corner, q, p, p_other, coupling, new_right, new_left):
    blocks, n, _ = q.shape
    half = blocks * n
    whole = lambda a: pl.BlockSpec(a.shape, lambda i, r: (0,) * a.ndim)
    return pl.pallas_call(
        prepare_kernel,
        out_shape=(
            jax.ShapeDtypeStruct((half, half), F32),
            jax.ShapeDtypeStruct((half, half), F32),
            jax.ShapeDtypeStruct(q.shape, F32),
            jax.ShapeDtypeStruct((3, n, n), F32),
        ),
        grid_spec=pltpu.PrefetchScalarGridSpec(
            num_scalar_prefetch=1,
            grid=(blocks,),
            in_specs=[
                pl.BlockSpec((n, half), lambda i, r: (i, r[0])),
                pl.BlockSpec((n, half), lambda i, r: (i, 1 - r[0])),
                pl.BlockSpec((1, n, n), lambda i, r: (i, 0, 0)),
                whole(p),
                whole(p_other),
                whole(coupling),
                whole(new_right),
                whole(new_left),
            ],
            out_specs=(
                pl.BlockSpec((n, half), lambda i, r: (i, 0)),
                pl.BlockSpec((n, half), lambda i, r: (i, 0)),
                pl.BlockSpec((1, n, n), lambda i, r: (i, 0, 0)),
                pl.BlockSpec((3, n, n), lambda i, r: (0, 0, 0)),
            ),
        ),
        name="prepare",
    )(row, corner, corner, q, p, p_other, coupling, new_right, new_left)


def chain_kernel(
    slots, lower, where, *refs
):
    rs, refs = refs[:slots], refs[slots:]
    if lower:
        (q_ref, t_ref, s_ref, p_ref, av_ref, bv_ref, g_ref, nr_ref, nl_ref, toff_ref,
         x_ref, w_ref, r_buf, c_buf) = refs
    else:
        (w_ref, q_ref, t_ref, s_ref, p_ref, av_ref, bv_ref, g_ref, nr_ref, nl_ref,
         x_ref, r_buf, c_buf) = refs
    blocks, n, _ = q_ref.shape
    for m in range(slots):
        r = rs[m][...]
        depth = r.shape[0]
        r_buf[pl.ds(pl.multiple_of((where[0] ^ m) * depth, 8), depth), :] = r
    nr0, nr1 = split(nr_ref[0]), split(nr_ref[1])
    left = slice(0, n)
    right = slice(n, 2 * n)

    def rows(i):
        return slice(i * n, (i + 1) * n)

    def start(i):
        qr = dot3(q_ref[i], r_buf[rows(i), :])
        c0 = dot3(qr[:, left], nr_ref[0])
        c1 = dot3(qr[:, right], nr_ref[1])
        if not lower:
            c0 = c0 - w_ref[rows(i), left]
            c1 = c1 - w_ref[rows(i), right]
        c_buf[rows(i), left] = c0
        c_buf[rows(i), right] = c1

    for i in range(blocks - 1, -1, -1):
        start(i)
    g0 = jnp.concatenate([g_ref[0], g_ref[1]], axis=1)
    g0, g1 = split(g0), split(g_ref[2])
    av = av_ref[...]

    def inverse(i, c):
        own = jnp.transpose(jnp.broadcast_to(av[i : i + 1, :], (n, n)))
        return 1.0 / (own + jnp.broadcast_to(bv_ref[c : c + 1, :], (n, n)))

    def finish(i, z0, z1):
        y = jnp.concatenate([dot3(z0, nl_ref[0]), dot3(z1, nl_ref[1])], axis=1)
        x_ref[rows(i), :] = dot3(p_ref[i], y)

    for i in range(blocks - 1, -1, -1):
        z0 = c_buf[rows(i), left] * inverse(i, 0)
        hj = dot_parts(split(z0), g0)
        h0 = split(hj[:, left])
        if i > 0:
            t = split(t_ref[rows(i - 1), rows(i)])
            c_buf[rows(i - 1), left] -= dot_parts(t, h0)
        z1 = (c_buf[rows(i), right] - dot3(s_ref[i], hj[:, right])) * inverse(i, 1)
        h1f = dot_parts(split(z1), g1)
        h1 = split(h1f)
        if i > 0:
            c_buf[rows(i - 1), right] -= dot_parts(t, h1)
        h = split(jnp.concatenate([hj[:, left], h1f], axis=1))
        if i > 1:
            above = slice(0, (i - 1) * n)
            c_buf[above, :] -= dot_parts(split(t_ref[above, rows(i)]), h)
        if lower:
            update = dot_parts(split(toff_ref[:, rows(i)]), h)
            if i == blocks - 1:
                w_ref[...] = update
            else:
                w_ref[...] += update
        finish(i, z0, z1)


def chain(where, r_parts, w, q, t, s, p, av, bv, g, nr, nl, toff):
    blocks, n, _ = q.shape
    lower = toff is not None
    slots = len(r_parts)
    shape = jax.ShapeDtypeStruct((blocks * n, 2 * n), F32)
    operands = list(r_parts) + ([] if lower else [w])
    operands += [q, t, s, p, av, bv, g, nr, nl] + ([toff] if lower else [])
    return pl.pallas_call(
        functools.partial(chain_kernel, slots, lower),
        out_shape=(shape, shape) if lower else shape,
        in_specs=[SMEM] + [VMEM] * len(operands),
        out_specs=(VMEM, VMEM) if lower else VMEM,
        scratch_shapes=[pltpu.VMEM(shape.shape, F32), pltpu.VMEM(shape.shape, F32)],
        name="chain_lower" if lower else "chain_upper",
    )(where, *operands)


def exchange(block, mask):
    route = [(i, i ^ mask) for i in range(lax.axis_size("col"))]
    return lax.ppermute(block, "col", route)


def swap_rows(block):
    return lax.ppermute(block, "row", [(0, 1), (1, 0)])


def shards(
    top_rows, lower_new, block_order, corner, target, coupling,
    top_right, top_left, top_values, new_right, new_left, new_values,
):
    cols = lax.axis_size("col")
    half_rows = target.shape[0]
    slots = min(cols, 8)
    depth = half_rows // slots
    row = lax.axis_index("row")
    where = lax.axis_index("col") % slots
    row_s, other_s, where_s = row[None], (1 - row)[None], where[None]

    theirs = partial_product(where_s, row_s, block_order, top_rows, lower_new, slots)
    theirs = swap_rows(theirs)
    ours = partial_product(where_s, other_s, block_order, top_rows, lower_new, slots)
    p_other = swap_rows(top_right)
    q_other = swap_rows(top_left)
    av_other = swap_rows(top_values)
    goal = swap_rows(lax.dynamic_slice_in_dim(target, where * depth, depth, 0))
    diag, toff, s, g = prepare(
        row_s, corner, top_left, top_right, p_other, coupling, new_right, new_left
    )
    diag_other = swap_rows(diag)
    s_other = swap_rows(s)

    pieces = [ours[m] + theirs[m] for m in range(slots)]
    total = pieces[0]
    for m in range(1, slots):
        total = total + exchange(pieces[m], m)
    mask = slots
    while mask < cols:
        total = total + exchange(total, mask)
        mask *= 2
    side = goal - total
    parts = [side] + [exchange(side, m) for m in range(1, slots)]
    upper_parts = swap_rows(jnp.stack(parts))

    x_lower, w = chain(
        where_s, parts, None, q_other, diag_other, s_other, p_other, av_other,
        new_values, g, new_right, new_left, toff,
    )
    x_lower = swap_rows(x_lower)
    x_upper = chain(
        where_s, [upper_parts[m] for m in range(slots)], w, top_left, diag, s, top_right,
        top_values, new_values, g, new_right, new_left, None,
    )
    return jnp.where(row == 0, x_upper, x_lower)


def solution(mesh):
    placed = (
        P(None, ("col", "row")),
        P(("col", "row"), None),
        P(("col", "row"), None),
        P("row", None),
        P("row", None),
        P(),
        P("row", None, None),
        P("row", None, None),
        P("row", None),
        P(),
        P(),
        P(),
    )
    return jax.shard_map(
        shards, mesh=mesh, in_specs=placed, out_specs=P("row", None), check_vma=False
    )
```

```python
import functools

import jax
import jax.numpy as jnp
from jax import lax
from jax.experimental import pallas as pl
from jax.experimental.pallas import tpu as pltpu
from jax.sharding import PartitionSpec as P


F32 = jnp.float32
BF16 = jnp.bfloat16
GRANT = 12 << 20

VMEM = pl.BlockSpec(memory_space=pltpu.VMEM)
SMEM = pl.BlockSpec(memory_space=pltpu.SMEM)


def split(x):
    high = x.astype(BF16)
    return high, (x - high.astype(F32)).astype(BF16)


def mm(a, b):
    return jnp.dot(a, b, preferred_element_type=F32)


def cat(parts, axis):
    return jnp.concatenate(parts, axis=axis)


def lhs(x):
    return cat(split(x), 1)


def wide_rhs(x):
    high, low = split(x)
    return cat([high, high], 0), low


def wide_dot(a, b):
    n = a.shape[1] // 2
    return mm(a, b[0]) + mm(a[:, :n], b[1])


def block_rhs(x):
    both = cat(split(x), 1)
    return cat([both, both], 0)


def block_dot(a, b):
    n = b.shape[1] // 2
    r = mm(a, b)
    return r[:, :n] + r[:, n:]


def params(**kw):
    return pltpu.CompilerParams(vmem_limit_bytes=GRANT, **kw)


def partial_kernel(where, half, order, a_ref, b_ref, out_ref):
    slots, depth, _ = out_ref.shape
    size = b_ref.shape[0] // order.shape[1]
    paired = [
        b_ref[pl.ds(pl.multiple_of(order[0, g] * size, size), size), :]
        for g in range(order.shape[1])
    ]
    high, low = split(cat(paired, 0))
    for m in range(slots):
        rows = (half[0] * slots + (where[0] ^ m)) * depth
        ah, al = split(a_ref[pl.ds(pl.multiple_of(rows, 8), depth), :])
        out_ref[m] = mm(ah, high) + (mm(ah, low) + mm(al, high))


def partial_product(where, half, order, top_rows, lower, slots):
    depth = top_rows.shape[0] // 2 // slots
    return pl.pallas_call(
        partial_kernel,
        out_shape=jax.ShapeDtypeStruct((slots, depth, lower.shape[1]), F32),
        in_specs=[SMEM, SMEM, SMEM, VMEM, VMEM],
        out_specs=VMEM,
        compiler_params=params(),
        name="partial_product",
    )(where, half, order, top_rows, lower)


def add_kernel(slots, a_ref, b_ref, *outs):
    for m in range(slots):
        outs[m][...] = a_ref[m] + b_ref[m]


def add_slots(a, b):
    slots = a.shape[0]
    shape = jax.ShapeDtypeStruct(a.shape[1:], F32)
    return pl.pallas_call(
        functools.partial(add_kernel, slots),
        out_shape=(shape,) * slots,
        in_specs=[VMEM, VMEM],
        out_specs=(VMEM,) * slots,
        compiler_params=params(),
        name="add_slots",
    )(a, b)


def sum_kernel(*refs):
    total = refs[0][...]
    for r in refs[1:-1]:
        total = total + r[...]
    refs[-1][...] = total


def sum_slots(*parts):
    return pl.pallas_call(
        sum_kernel,
        out_shape=jax.ShapeDtypeStruct(parts[0].shape, F32),
        in_specs=[VMEM] * len(parts),
        out_specs=VMEM,
        compiler_params=params(),
        name="sum_slots",
    )(*parts)


def side_kernel(*refs):
    goal, nr, out = refs[-3:]
    total = refs[0][...]
    for r in refs[1:-3]:
        total = total + r[...]
    side = goal[...] - total
    n = nr.shape[1]
    for c in range(2):
        cols = slice(c * n, (c + 1) * n)
        out[:, cols] = block_dot(lhs(side[:, cols]), block_rhs(nr[c]))


def side_slot(parts, goal, new_right):
    return pl.pallas_call(
        side_kernel,
        out_shape=jax.ShapeDtypeStruct(goal.shape, F32),
        in_specs=[VMEM] * (len(parts) + 2),
        out_specs=VMEM,
        compiler_params=params(),
        name="side_slot",
    )(*parts, goal, new_right)


def rotate_kernel(slots, where, *refs):
    rs, (q_ref, out, buf) = refs[:slots], refs[slots:]
    blocks, n, _ = q_ref.shape
    for m in range(slots):
        depth = rs[m].shape[0]
        buf[pl.ds(pl.multiple_of((where[0] ^ m) * depth, 8), depth), :] = rs[m][...]
    for i in range(blocks):
        rows = slice(i * n, (i + 1) * n)
        out[rows, :] = wide_dot(lhs(q_ref[i]), wide_rhs(buf[rows, :]))


def rotate(where, parts, q):
    blocks, n, _ = q.shape
    shape = (blocks * n, parts[0].shape[1])
    return pl.pallas_call(
        functools.partial(rotate_kernel, len(parts)),
        out_shape=jax.ShapeDtypeStruct(shape, F32),
        in_specs=[SMEM] + [VMEM] * (len(parts) + 1),
        out_specs=VMEM,
        scratch_shapes=[pltpu.VMEM(shape, F32)],
        compiler_params=params(),
        name="rotate",
    )(where, *parts, q)


def own_kernel(row, u_ref, q_ref, p_ref, e_ref, nr_ref, nl_ref, diag_ref, s_ref, g_ref):
    blocks, n, _ = p_ref.shape
    p = [block_rhs(p_ref[k]) for k in range(blocks)]
    for i in range(blocks):
        q = lhs(q_ref[i])
        rows = slice(i * n, (i + 1) * n)
        s_ref[i] = block_dot(q, p[i])
        if i > 0:
            diag_ref[rows, : i * n] = jnp.zeros((n, i * n), F32)
        diag_ref[rows, i * n : (i + 1) * n] = jnp.zeros((n, n), F32)
        if i + 1 < blocks:
            qu = wide_dot(q, wide_rhs(u_ref[rows, (i + 1) * n :]))
        for k in range(i + 1, blocks):
            own = qu[:, (k - i - 1) * n : (k - i) * n]
            diag_ref[rows, k * n : (k + 1) * n] = block_dot(lhs(own), p[k])
    left = lhs(nl_ref[0])
    g_ref[0] = block_dot(left, block_rhs(nr_ref[0]))
    both = block_dot(left, block_rhs(e_ref[...]))
    g_ref[1] = block_dot(lhs(both), block_rhs(nr_ref[1]))
    g_ref[2] = block_dot(lhs(nl_ref[1]), block_rhs(nr_ref[1]))


def whole(a):
    return pl.BlockSpec(a.shape, lambda i, r: (0,) * a.ndim)


def prepare_own(row, corner, q, p, coupling, new_right, new_left):
    blocks, n, _ = q.shape
    half = blocks * n
    shapes = (
        jax.ShapeDtypeStruct((half, half), F32),
        jax.ShapeDtypeStruct(q.shape, F32),
        jax.ShapeDtypeStruct((3, n, n), F32),
    )
    return pl.pallas_call(
        own_kernel,
        out_shape=shapes,
        grid_spec=pltpu.PrefetchScalarGridSpec(
            num_scalar_prefetch=1,
            grid=(1,),
            in_specs=[
                pl.BlockSpec((half, half), lambda i, r: (0, r[0])),
                whole(q),
                whole(p),
                whole(coupling),
                whole(new_right),
                whole(new_left),
            ],
            out_specs=tuple(whole(a) for a in shapes),
        ),
        compiler_params=params(),
        name="prepare_own",
    )(row, corner, q, p, coupling, new_right, new_left)


def cross_kernel(row, u_ref, q_ref, p_ref, out_ref):
    blocks, n, _ = p_ref.shape
    q = lhs(q_ref[0])
    for k in range(0, blocks, 2):
        last = min(k + 2, blocks)
        u = u_ref[:, k * n : last * n]
        if last - k == 2:
            qu = wide_dot(q, wide_rhs(u))
        else:
            qu = block_dot(q, block_rhs(u))
        for j in range(k, last):
            own = lhs(qu[:, (j - k) * n : (j - k + 1) * n])
            out_ref[j] = lhs(block_dot(own, block_rhs(p_ref[j])))


def prepare_cross(row, corner, q, p_other):
    blocks, n, _ = q.shape
    half = blocks * n
    return pl.pallas_call(
        cross_kernel,
        out_shape=jax.ShapeDtypeStruct((blocks, half, 2 * n), BF16),
        grid_spec=pltpu.PrefetchScalarGridSpec(
            num_scalar_prefetch=1,
            grid=(blocks,),
            in_specs=[
                pl.BlockSpec((n, half), lambda i, r: (i, 1 - r[0])),
                pl.BlockSpec((1, n, n), lambda i, r: (i, 0, 0)),
                whole(p_other),
            ],
            out_specs=pl.BlockSpec((blocks, n, 2 * n), lambda i, r: (0, i, 0)),
        ),
        compiler_params=params(),
        name="prepare_cross",
    )(row, corner, q, p_other)


def chain_kernel(lower, *refs):
    if lower:
        c_ref, t_ref, s_ref, av_ref, bv_ref, g_ref, toff_ref, z_ref, w_ref, c_buf = refs
    else:
        c_ref, w_ref, t_ref, s_ref, av_ref, bv_ref, g_ref, z_ref, c_buf = refs
    blocks, n, _ = s_ref.shape
    left = slice(0, n)
    right = slice(n, 2 * n)

    def rows(i):
        return slice(i * n, (i + 1) * n)

    g0 = wide_rhs(cat([g_ref[0], g_ref[1]], 1))
    g1 = block_rhs(g_ref[2])
    av = av_ref[...]

    def inverse(i, c):
        own = jnp.transpose(jnp.broadcast_to(av[i : i + 1, :], (n, n)))
        return 1.0 / (own + jnp.broadcast_to(bv_ref[c : c + 1, :], (n, n)))

    if lower:
        c_buf[...] = c_ref[...]
    else:
        c_buf[...] = c_ref[...] - w_ref[...]
    for i in range(blocks - 1, -1, -1):
        z0 = c_buf[rows(i), left] * inverse(i, 0)
        z_ref[rows(i), left] = z0
        hj = wide_dot(lhs(z0), g0)
        h0 = hj[:, left]
        if i > 0:
            t = lhs(t_ref[rows(i - 1), rows(i)])
            c_buf[rows(i - 1), left] -= block_dot(t, block_rhs(h0))
        coupled = block_dot(lhs(s_ref[i]), block_rhs(hj[:, right]))
        z1 = (c_buf[rows(i), right] - coupled) * inverse(i, 1)
        z_ref[rows(i), right] = z1
        h1 = block_dot(lhs(z1), g1)
        if i > 0:
            c_buf[rows(i - 1), right] -= block_dot(t, block_rhs(h1))
        if lower or i > 1:
            h = wide_rhs(cat([h0, h1], 1))
        if i > 1:
            above = slice(0, (i - 1) * n)
            c_buf[above, :] -= wide_dot(lhs(t_ref[above, rows(i)]), h)
        if lower:
            update = wide_dot(toff_ref[i], h)
            if i == blocks - 1:
                w_ref[...] = update
            else:
                w_ref[...] += update


def chain(c, w, t, s, av, bv, g, toff):
    blocks, n, _ = s.shape
    lower = toff is not None
    shape = jax.ShapeDtypeStruct((blocks * n, 2 * n), F32)
    operands = [c] + ([] if lower else [w])
    operands += [t, s, av, bv, g] + ([toff] if lower else [])
    return pl.pallas_call(
        functools.partial(chain_kernel, lower),
        out_shape=(shape, shape) if lower else shape,
        in_specs=[VMEM] * len(operands),
        out_specs=(VMEM, VMEM) if lower else VMEM,
        scratch_shapes=[pltpu.VMEM(shape.shape, F32)],
        compiler_params=params(),
        name="chain_lower" if lower else "chain_upper",
    )(*operands)


def final_kernel(row, upper_ref, lower_ref, p_ref, nl_ref, out_ref):
    blocks, n, _ = p_ref.shape
    nl = [block_rhs(nl_ref[c]) for c in range(2)]

    def solve(z_ref):
        for i in range(blocks):
            rows = slice(i * n, (i + 1) * n)
            y = [
                block_dot(lhs(z_ref[rows, c * n : (c + 1) * n]), nl[c]) for c in range(2)
            ]
            out_ref[rows, :] = wide_dot(lhs(p_ref[i]), wide_rhs(cat(y, 1)))

    @pl.when(row[0] == 0)
    def _():
        solve(upper_ref)

    @pl.when(row[0] != 0)
    def _():
        solve(lower_ref)


def final(row, z_upper, z_lower, p, new_left):
    return pl.pallas_call(
        final_kernel,
        out_shape=jax.ShapeDtypeStruct(z_upper.shape, F32),
        in_specs=[SMEM] + [VMEM] * 4,
        out_specs=VMEM,
        compiler_params=params(),
        name="final",
    )(row, z_upper, z_lower, p, new_left)


def exchange(block, mask):
    route = [(i, i ^ mask) for i in range(lax.axis_size("col"))]
    return lax.ppermute(block, "col", route)


def swap_rows(block):
    return lax.ppermute(block, "row", [(0, 1), (1, 0)])


def body(
    top_rows, lower_new, block_order, corner, target, coupling,
    top_right, top_left, top_values, new_right, new_left, new_values,
):
    cols = lax.axis_size("col")
    half_rows = target.shape[0]
    slots = min(cols, 8)
    depth = half_rows // slots
    row = lax.axis_index("row")
    where = lax.axis_index("col") % slots
    row_s, other_s, where_s = row[None], (1 - row)[None], where[None]

    corner = pltpu.with_memory_space_constraint(corner, pltpu.HBM)
    theirs = partial_product(where_s, row_s, block_order, top_rows, lower_new, slots)
    theirs = swap_rows(theirs)
    ours = partial_product(where_s, other_s, block_order, top_rows, lower_new, slots)
    pieces = add_slots(ours, theirs)
    received = [exchange(pieces[m], m) for m in range(1, slots)]
    diag, s, g = prepare_own(
        row_s, corner, top_left, top_right, coupling, new_right, new_left
    )
    p_other = swap_rows(top_right)
    q_other = swap_rows(top_left)
    av_other = swap_rows(top_values)
    goal = swap_rows(lax.dynamic_slice_in_dim(target, where * depth, depth, 0))
    toff = prepare_cross(row_s, corner, top_left, p_other)
    diag_other = swap_rows(diag)
    s_other = swap_rows(s)

    total = sum_slots(pieces[0], *received)
    mask = slots
    last = []
    while mask < cols:
        moved = exchange(total, mask)
        if mask * 2 < cols:
            total = total + moved
        else:
            last = [moved]
        mask *= 2
    side = side_slot([total] + last, goal, new_right)
    parts = [side] + [exchange(side, m) for m in range(1, slots)]
    c_lower = rotate(where_s, parts, q_other)
    c_upper = swap_rows(c_lower)
    z_lower, w = chain(
        c_lower, None, diag_other, s_other, av_other, new_values, g, toff
    )
    z_lower = swap_rows(z_lower)
    z_upper = chain(c_upper, w, diag, s, top_values, new_values, g, None)
    return final(row_s, z_upper, z_lower, top_right, new_left)


def solution(mesh):
    placed = (
        P(None, ("col", "row")),
        P(("col", "row"), None),
        P(("col", "row"), None),
        P("row", None),
        P("row", None),
        P(),
        P("row", None, None),
        P("row", None, None),
        P("row", None),
        P(),
        P(),
        P(),
    )
    return jax.shard_map(
        body, mesh=mesh, in_specs=placed, out_specs=P("row", None), check_vma=False
    )
```

```python
import functools

import jax
import jax.numpy as jnp
from jax import lax
from jax.experimental import pallas as pl
from jax.experimental.pallas import tpu as pltpu
from jax.sharding import PartitionSpec as P


F32 = jnp.float32
BF16 = jnp.bfloat16
GRANT = 12 << 20

VMEM = pl.BlockSpec(memory_space=pltpu.VMEM)
SMEM = pl.BlockSpec(memory_space=pltpu.SMEM)
HBM = pl.BlockSpec(memory_space=pltpu.HBM)


def split(x):
    high = x.astype(BF16)
    return high, (x - high.astype(F32)).astype(BF16)


def mm(a, b):
    return jnp.dot(a, b, preferred_element_type=F32)


def cat(parts, axis):
    return jnp.concatenate(parts, axis=axis)


def lhs(x):
    return cat(split(x), 1)


def wide_rhs(x):
    high, low = split(x)
    return cat([high, high], 0), low


def wide_dot(a, b):
    n = a.shape[1] // 2
    return mm(a, b[0]) + mm(a[:, :n], b[1])


def block_rhs(x):
    both = cat(split(x), 1)
    return cat([both, both], 0)


def block_dot(a, b):
    n = b.shape[1] // 2
    r = mm(a, b)
    return r[:, :n] + r[:, n:]


def params(**kw):
    return pltpu.CompilerParams(vmem_limit_bytes=GRANT, **kw)


def place(slots):
    return lax.axis_index("row"), lax.axis_index("col") % slots


def partial_kernel(own, order_hbm, a_hbm, b_hbm, *refs):
    small, refs = (refs[:5], refs[5:]) if not own else ((), refs)
    out_ref, refs = refs[0], refs[1:]
    const_ref, refs = (refs[0], refs[1:]) if not own else (None, refs)
    order, a_buf, b_buf, sems = refs
    slots, depth, _ = out_ref.shape
    groups = order.shape[1]
    size = b_buf.shape[0] // groups
    row, where = place(slots)
    half = 1 - row if own else row
    copies = [
        pltpu.make_async_copy(order_hbm, order, sems.at[slots]),
        pltpu.make_async_copy(b_hbm, b_buf, sems.at[slots + 1]),
    ]
    for m in range(slots):
        rows = pl.multiple_of((half * slots + (where ^ m)) * depth, 8)
        copies.append(
            pltpu.make_async_copy(a_hbm.at[pl.ds(rows, depth)], a_buf.at[m], sems.at[m])
        )
    if not own:
        _, _, _, av, bv = small
        targets = (
            const_ref.at[pl.ds(0, 2)],
            const_ref.at[pl.ds(2, 2)],
            const_ref.at[4],
            const_ref.at[5, pl.ds(0, av.shape[0])],
            const_ref.at[6, pl.ds(0, bv.shape[0])],
        )
        for j, (source, target) in enumerate(zip(small, targets)):
            copies.append(pltpu.make_async_copy(source, target, sems.at[slots + 2 + j]))
    for copy in copies:
        copy.start()
    copies[0].wait()
    copies[1].wait()
    paired = [
        b_buf[pl.ds(pl.multiple_of(order[0, g] * size, size), size), :]
        for g in range(groups)
    ]
    high, low = split(cat(paired, 0))
    for m in range(slots):
        copies[2 + m].wait()
        ah, al = split(a_buf[m])
        out_ref[m] = mm(ah, high) + (mm(ah, low) + mm(al, high))
    for copy in copies[2 + slots :]:
        copy.wait()


def partial_product(order, top_rows, lower, slots, small=None):
    own = small is None
    depth, inner = top_rows.shape[0] // 2 // slots, top_rows.shape[1]
    out = jax.ShapeDtypeStruct((slots, depth, lower.shape[1]), F32)
    operands = (order, top_rows, lower) + (() if own else small)
    if not own:
        out = (out, jax.ShapeDtypeStruct((7,) + small[2].shape, F32))
    return pl.pallas_call(
        functools.partial(partial_kernel, own),
        out_shape=out,
        in_specs=[HBM] * len(operands),
        out_specs=VMEM if own else (VMEM, VMEM),
        scratch_shapes=[
            pltpu.SMEM(order.shape, jnp.int32),
            pltpu.VMEM((slots, depth, inner), F32),
            pltpu.VMEM(lower.shape, F32),
            pltpu.SemaphoreType.DMA((slots + 7,)),
        ],
        compiler_params=params(),
        name="partial_own" if own else "partial_other",
    )(*operands)


def add_kernel(slots, a_ref, b_ref, *outs):
    for m in range(slots):
        outs[m][...] = a_ref[m] + b_ref[m]


def add_slots(a, b):
    slots = a.shape[0]
    shape = pltpu.VMEM(a.shape[1:], F32)
    return pl.pallas_call(
        functools.partial(add_kernel, slots),
        out_shape=(shape,) * slots,
        in_specs=[VMEM, VMEM],
        out_specs=(VMEM,) * slots,
        compiler_params=params(),
        name="add_slots",
    )(a, b)


def sum_kernel(*refs):
    total = refs[0][...]
    for r in refs[1:-1]:
        total = total + r[...]
    refs[-1][...] = total


def sum_slots(*parts):
    return pl.pallas_call(
        sum_kernel,
        out_shape=jax.ShapeDtypeStruct(parts[0].shape, F32),
        in_specs=[VMEM] * len(parts),
        out_specs=VMEM,
        compiler_params=params(),
        name="sum_slots",
    )(*parts)


def side_kernel(*refs):
    goal, const, out = refs[-3:]
    total = refs[0][...]
    for r in refs[1:-3]:
        total = total + r[...]
    side = goal[...] - total
    n = const.shape[1]
    for c in range(2):
        cols = slice(c * n, (c + 1) * n)
        out[:, cols] = block_dot(lhs(side[:, cols]), block_rhs(const[c]))


def side_slot(parts, goal, const):
    return pl.pallas_call(
        side_kernel,
        out_shape=jax.ShapeDtypeStruct(goal.shape, F32),
        in_specs=[VMEM] * (len(parts) + 2),
        out_specs=VMEM,
        compiler_params=params(),
        name="side_slot",
    )(*parts, goal, const)


def stage_kernel(*refs):
    count = len(refs) // 2
    sems = refs[-1]
    copies = [
        pltpu.make_async_copy(refs[j], refs[count + j], sems.at[j]) for j in range(count)
    ]
    for copy in copies:
        copy.start()
    for copy in copies:
        copy.wait()


def stage(*arrays):
    return pl.pallas_call(
        stage_kernel,
        out_shape=tuple(jax.ShapeDtypeStruct(a.shape, F32) for a in arrays),
        in_specs=[HBM] * len(arrays),
        out_specs=(VMEM,) * len(arrays),
        scratch_shapes=[pltpu.SemaphoreType.DMA((len(arrays),))],
        compiler_params=params(),
        name="stage",
    )(*arrays)


def rotate_kernel(slots, *refs):
    rs, (q_ref, out, buf) = refs[:slots], refs[slots:]
    blocks, n, _ = q_ref.shape
    _, where = place(slots)
    for m in range(slots):
        depth = rs[m].shape[0]
        buf[pl.ds(pl.multiple_of((where ^ m) * depth, 8), depth), :] = rs[m][...]
    for i in range(blocks):
        rows = slice(i * n, (i + 1) * n)
        out[rows, :] = wide_dot(lhs(q_ref[i]), wide_rhs(buf[rows, :]))


def rotate(parts, q):
    blocks, n, _ = q.shape
    shape = (blocks * n, parts[0].shape[1])
    return pl.pallas_call(
        functools.partial(rotate_kernel, len(parts)),
        out_shape=jax.ShapeDtypeStruct(shape, F32),
        in_specs=[VMEM] * (len(parts) + 1),
        out_specs=VMEM,
        scratch_shapes=[pltpu.VMEM(shape, F32)],
        compiler_params=params(),
        name="rotate",
    )(*parts, q)


def first_block(k):
    return k * (k - 1) // 2


def prepare_kernel(u_hbm, q_hbm, p_hbm, const, out_ref, u_buf, q_buf, p_buf, sems):
    blocks, n, _ = p_buf.shape
    row = lax.axis_index("row")
    base = first_block(blocks)
    copies = [
        pltpu.make_async_copy(q_hbm, q_buf, sems.at[blocks]),
        pltpu.make_async_copy(p_hbm, p_buf, sems.at[blocks + 1]),
    ]
    for i in range(blocks - 1):
        first, count = (i + 1) * n, (blocks - 1 - i) * n
        cols = pl.multiple_of(row * (blocks * n) + first, n)
        copies.append(
            pltpu.make_async_copy(
                u_hbm.at[pl.ds(i * n, n), pl.ds(cols, count)],
                u_buf.at[pl.ds(i * n, n), pl.ds(first, count)],
                sems.at[i],
            )
        )
    for copy in copies:
        copy.start()
    left = lhs(const[2])
    out_ref[base + 2 * blocks] = block_dot(left, block_rhs(const[0]))
    both = block_dot(left, block_rhs(const[4]))
    out_ref[base + 2 * blocks + 1] = block_dot(lhs(both), block_rhs(const[1]))
    out_ref[base + 2 * blocks + 2] = block_dot(lhs(const[3]), block_rhs(const[1]))
    out_ref[base + 2 * blocks + 3, :blocks] = const[5, :blocks]
    for copy in copies[:2]:
        copy.wait()
    p = [block_rhs(p_buf[k]) for k in range(blocks)]
    out_ref[base + blocks : base + 2 * blocks] = p_buf[...]
    for i in range(blocks):
        q = lhs(q_buf[i])
        out_ref[base + i] = block_dot(q, p[i])
        if i + 1 == blocks:
            break
        copies[2 + i].wait()
        qu = wide_dot(q, wide_rhs(u_buf[i * n : (i + 1) * n, (i + 1) * n :]))
        for k in range(i + 1, blocks):
            own = qu[:, (k - i - 1) * n : (k - i) * n]
            out_ref[first_block(k) + i] = block_dot(lhs(own), p[k])


def prepare(corner, q, p, const):
    blocks, n, _ = q.shape
    count = first_block(blocks) + 2 * blocks + 4
    return pl.pallas_call(
        prepare_kernel,
        out_shape=jax.ShapeDtypeStruct((count, n, n), F32),
        in_specs=[HBM, HBM, HBM, VMEM],
        out_specs=VMEM,
        scratch_shapes=[
            pltpu.VMEM((blocks * n, blocks * n), F32),
            pltpu.VMEM(q.shape, F32),
            pltpu.VMEM(p.shape, F32),
            pltpu.SemaphoreType.DMA((blocks + 2,)),
        ],
        compiler_params=params(),
        name="prepare",
    )(corner, q, p, const)


def cross_kernel(first, u_hbm, q_hbm, t_hbm, out_ref, u_buf, q_buf, p_buf, sems):
    blocks, n, _ = p_buf.shape
    count = q_buf.shape[0]
    base = first_block(blocks) + blocks

    @pl.when(lax.axis_index("row") == 0)
    def _():
        copies = [
            pltpu.make_async_copy(
                t_hbm.at[pl.ds(base, blocks)], p_buf, sems.at[count]
            ),
            pltpu.make_async_copy(q_hbm.at[pl.ds(first, count)], q_buf, sems.at[count + 1]),
        ]
        for i in range(count):
            copies.append(
                pltpu.make_async_copy(
                    u_hbm.at[pl.ds((first + i) * n, n), pl.ds(blocks * n, blocks * n)],
                    u_buf.at[pl.ds(i * n, n)],
                    sems.at[i],
                )
            )
        for copy in copies:
            copy.start()
        for copy in copies[:2]:
            copy.wait()
        p = [block_rhs(p_buf[k]) for k in range(blocks)]
        for i in range(count):
            copies[2 + i].wait()
            rows = slice(i * n, (i + 1) * n)
            qu = wide_dot(lhs(q_buf[i]), wide_rhs(u_buf[rows, :]))
            for k in range(blocks):
                own = lhs(qu[:, k * n : (k + 1) * n])
                out_ref[k, rows, :] = lhs(block_dot(own, p[k]))


def prepare_cross(first, last, corner, q, shipped):
    blocks, n, _ = q.shape
    count = last - first
    return pl.pallas_call(
        functools.partial(cross_kernel, first),
        out_shape=jax.ShapeDtypeStruct((blocks, count * n, 2 * n), BF16),
        in_specs=[HBM, HBM, HBM],
        out_specs=VMEM,
        scratch_shapes=[
            pltpu.VMEM((count * n, blocks * n), F32),
            pltpu.VMEM((count,) + q.shape[1:], F32),
            pltpu.VMEM(q.shape, F32),
            pltpu.SemaphoreType.DMA((count + 2,)),
        ],
        compiler_params=params(),
    )(corner, q, shipped)


def chain_kernel(lower, *refs):
    if lower:
        c_ref, t_ref, const, z_ref, h_ref, c_buf = refs
    else:
        c_ref, w_ref, t_ref, const, z_ref, c_buf = refs
    row = lax.axis_index("row")
    n = t_ref.shape[1]
    blocks = c_ref.shape[0] // n
    base = first_block(blocks)
    left = slice(0, n)
    right = slice(n, 2 * n)

    def rows(i):
        return slice(i * n, (i + 1) * n)

    @pl.when(row == 0)
    def _():
        bv = const[6, :8]
        gs = [t_ref[base + 2 * blocks + j] for j in range(3)]
        g0 = wide_rhs(cat(gs[:2], 1))
        g1 = block_rhs(gs[2])
        av = t_ref[base + 2 * blocks + 3, : 8 * ((blocks + 7) // 8), :]

        def inverse(i, c):
            own = jnp.transpose(jnp.broadcast_to(av[i : i + 1, :], (n, n)))
            return 1.0 / (own + jnp.broadcast_to(bv[c : c + 1, :], (n, n)))

        if lower:
            c_buf[...] = c_ref[...]
        else:
            c_buf[...] = c_ref[...] - w_ref[...]
        for i in range(blocks - 1, -1, -1):
            z0 = c_buf[rows(i), left] * inverse(i, 0)
            z_ref[rows(i), left] = z0
            hj = wide_dot(lhs(z0), g0)
            h0 = hj[:, left]
            if i > 0:
                t = lhs(t_ref[first_block(i) + i - 1])
                c_buf[rows(i - 1), left] -= block_dot(t, block_rhs(h0))
            coupled = block_dot(lhs(t_ref[base + i]), block_rhs(hj[:, right]))
            z1 = (c_buf[rows(i), right] - coupled) * inverse(i, 1)
            z_ref[rows(i), right] = z1
            if lower or i > 0:
                h1 = block_dot(lhs(z1), g1)
            if i > 0:
                c_buf[rows(i - 1), right] -= block_dot(t, block_rhs(h1))
            if lower:
                h_ref[rows(i), left] = h0
                h_ref[rows(i), right] = h1
            if i > 1:
                h = wide_rhs(cat([h0, h1], 1))
                above = t_ref[first_block(i) : first_block(i) + i - 1]
                above = lhs(above.reshape((i - 1) * n, n))
                c_buf[: (i - 1) * n, :] -= wide_dot(above, h)

    if lower:

        @pl.when(row != 0)
        def _():
            z_ref[...] = c_ref[...]


def chain(c, w, t, const):
    lower = w is None
    shape = jax.ShapeDtypeStruct(c.shape, F32)
    operands = [c] + ([] if lower else [w]) + [t, const]
    return pl.pallas_call(
        functools.partial(chain_kernel, lower),
        out_shape=(shape, shape) if lower else shape,
        in_specs=[VMEM] * len(operands),
        out_specs=(VMEM, VMEM) if lower else VMEM,
        scratch_shapes=[pltpu.VMEM(shape.shape, F32)],
        compiler_params=params(),
        name="chain_lower" if lower else "chain_upper",
    )(*operands)


def apply_kernel(*refs):
    toffs, (h_ref, w_ref) = refs[:-2], refs[-2:]
    blocks, _, wide = toffs[0].shape
    n = wide // 2

    @pl.when(lax.axis_index("row") == 0)
    def _():
        hs = [wide_rhs(h_ref[k * n : (k + 1) * n, :]) for k in range(blocks)]
        first = 0
        for toff in toffs:
            total = wide_dot(toff[0], hs[0])
            for k in range(1, blocks):
                total = total + wide_dot(toff[k], hs[k])
            w_ref[first : first + toff.shape[1], :] = total
            first += toff.shape[1]


def apply_cross(toffs, h):
    return pl.pallas_call(
        apply_kernel,
        out_shape=jax.ShapeDtypeStruct(h.shape, F32),
        in_specs=[VMEM] * (len(toffs) + 1),
        out_specs=VMEM,
        compiler_params=params(),
        name="apply_cross",
    )(*toffs, h)


def final_kernel(upper_ref, lower_ref, t_ref, const, out_ref):
    n = t_ref.shape[1]
    blocks = out_ref.shape[0] // n
    base = first_block(blocks) + blocks
    nl = [block_rhs(const[2 + c]) for c in range(2)]

    def solve(z_ref):
        for i in range(blocks):
            rows = slice(i * n, (i + 1) * n)
            y = [
                block_dot(lhs(z_ref[rows, c * n : (c + 1) * n]), nl[c]) for c in range(2)
            ]
            out_ref[rows, :] = wide_dot(lhs(t_ref[base + i]), wide_rhs(cat(y, 1)))

    @pl.when(lax.axis_index("row") == 0)
    def _():
        solve(upper_ref)

    @pl.when(lax.axis_index("row") != 0)
    def _():
        solve(lower_ref)


def final(z_upper, z_lower, packed, const):
    return pl.pallas_call(
        final_kernel,
        out_shape=jax.ShapeDtypeStruct(z_upper.shape, F32),
        in_specs=[VMEM] * 4,
        out_specs=VMEM,
        compiler_params=params(),
        name="final",
    )(z_upper, z_lower, packed, const)


def exchange(block, mask):
    route = [(i, i ^ mask) for i in range(lax.axis_size("col"))]
    return lax.ppermute(block, "col", route)


def swap_rows(block):
    return lax.ppermute(block, "row", [(0, 1), (1, 0)])


def far(x):
    return pltpu.with_memory_space_constraint(x, pltpu.HBM)


def body(
    top_rows, lower_new, block_order, corner, target, coupling,
    top_right, top_left, top_values, new_right, new_left, new_values,
):
    cols = lax.axis_size("col")
    half_rows = target.shape[0]
    slots = min(cols, 8)
    depth = half_rows // slots
    where = lax.axis_index("col") % slots
    small = (new_right, new_left, coupling, top_values, new_values)
    small = tuple(map(far, small))
    block_order, top_rows, lower_new, corner, top_left, top_right = map(
        far, (block_order, top_rows, lower_new, corner, top_left, top_right)
    )

    theirs, const = partial_product(block_order, top_rows, lower_new, slots, small)
    theirs = swap_rows(theirs)
    ours = partial_product(block_order, top_rows, lower_new, slots)
    q_other = far(swap_rows(top_left))
    goal = swap_rows(lax.dynamic_slice_in_dim(target, where * depth, depth, 0))
    pieces = add_slots(ours, theirs)
    received = [exchange(pieces[m], m) for m in range(1, slots)]
    packed = prepare(corner, top_left, top_right, const)
    shipped = far(swap_rows(packed))
    blocks = top_left.shape[0]
    cut = blocks * 3 // 7
    toffs = (
        prepare_cross(0, cut, corner, top_left, shipped),
        prepare_cross(cut, blocks, corner, top_left, shipped),
    )
    near, q_near = stage(shipped, q_other)

    total = sum_slots(pieces[0], *received)
    mask = slots
    last = []
    while mask < cols:
        moved = exchange(total, mask)
        if mask * 2 < cols:
            total = total + moved
        else:
            last = [moved]
        mask *= 2
    side = side_slot([total] + last, goal, const)
    parts = [side] + [exchange(side, m) for m in range(1, slots)]
    c_own = rotate(parts, q_near)
    z_lower, h = chain(c_own, None, near, const)
    moved = swap_rows(z_lower)
    w = apply_cross(toffs, h)
    z_upper = chain(moved, w, packed, const)
    return final(z_upper, moved, packed, const)


def solution(mesh):
    placed = (
        P(None, ("col", "row")),
        P(("col", "row"), None),
        P(("col", "row"), None),
        P("row", None),
        P("row", None),
        P(),
        P("row", None, None),
        P("row", None, None),
        P("row", None),
        P(),
        P(),
        P(),
    )
    return jax.shard_map(
        body, mesh=mesh, in_specs=placed, out_specs=P("row", None), check_vma=False
    )
```

```python
import functools

import jax
import jax.numpy as jnp
from jax import lax
from jax.experimental import pallas as pl
from jax.experimental.pallas import tpu as pltpu
from jax.sharding import PartitionSpec as P


F32 = jnp.float32
BF16 = jnp.bfloat16
GRANT = 12 << 20

VMEM = pl.BlockSpec(memory_space=pltpu.VMEM)
SMEM = pl.BlockSpec(memory_space=pltpu.SMEM)
HBM = pl.BlockSpec(memory_space=pltpu.HBM)


def split(x):
    high = x.astype(BF16)
    return high, (x - high.astype(F32)).astype(BF16)


def mm(a, b):
    return jnp.dot(a, b, preferred_element_type=F32)


def cat(parts, axis):
    return jnp.concatenate(parts, axis=axis)


def lhs(x):
    return cat(split(x), 1)


def wide_rhs(x):
    high, low = split(x)
    return cat([high, high], 0), low


def wide_dot(a, b):
    n = a.shape[1] // 2
    return mm(a, b[0]) + mm(a[:, :n], b[1])


def block_rhs(x):
    both = cat(split(x), 1)
    return cat([both, both], 0)


def block_dot(a, b):
    n = b.shape[1] // 2
    r = mm(a, b)
    return r[:, :n] + r[:, n:]


def params(**kw):
    return pltpu.CompilerParams(vmem_limit_bytes=GRANT, **kw)


def orders(slots):
    rows = ((0, 4, 3, 7, 5, 6, 1, 2), (0, 3, 4, 1, 5, 2, 6, 7))
    return tuple(tuple(m for m in masks if m < slots) for masks in rows)


def mask_at(slots, row, k):
    first, second = (masks[k] for masks in orders(slots))
    return first + row * (second - first)


def device_mask(cols, row, mask):
    if row == 1 and cols >= 16 and mask & 4:
        return (mask & 3) | 12
    return mask


def last_masks(cols, row):
    slots = min(cols, 8)
    masks = [slots << k for k in range((cols // slots).bit_length() - 1)]
    if row == 1 and cols >= 16:
        masks[0] = 4
    return masks


def position(row, slots):
    col = lax.axis_index("col")
    first = col & (slots - 1)
    if lax.axis_size("col") < 16:
        return first
    second = (col & 3) | (((col >> 3) & 1) << 2)
    return first + row * (second - first)


def group(row):
    col = lax.axis_index("col")
    if lax.axis_size("col") < 16:
        return col & 0
    second = ((col >> 4) << 1) | (((col >> 2) ^ (col >> 3)) & 1)
    first = col >> 3
    return first + row * (second - first)


def partial_kernel(own, order_hbm, a_hbm, b_hbm, *refs):
    small, refs = (refs[:6], refs[6:]) if not own else ((), refs)
    out_ref, refs = refs[0], refs[1:]
    const_ref, refs = (refs[0], refs[1:]) if not own else (None, refs)
    order, a_buf, b_buf, sems, goal = refs
    slots, depth, _ = out_ref.shape
    groups = order.shape[1]
    size = b_buf.shape[0] // groups
    row = lax.axis_index("row")
    half = 1 - row if own else row
    where = position(1 - half, slots)
    copies = [
        pltpu.make_async_copy(order_hbm, order, sems.at[slots]),
        pltpu.make_async_copy(b_hbm, b_buf, sems.at[slots + 1]),
    ]
    for m in range(slots):
        slot = where ^ mask_at(slots, 1 - half, m)
        rows = pl.multiple_of((half * slots + slot) * depth, 8)
        copies.append(
            pltpu.make_async_copy(a_hbm.at[pl.ds(rows, depth)], a_buf.at[m], sems.at[m])
        )
    if not own:
        target, _, _, _, av, bv = small
        goal_rows = pl.multiple_of(where * depth, 8)
        targets = (
            const_ref.at[pl.ds(0, 2)],
            const_ref.at[pl.ds(2, 2)],
            const_ref.at[4],
            const_ref.at[5, pl.ds(0, av.shape[0])],
            const_ref.at[6, pl.ds(0, bv.shape[0])],
        )
        targets += (goal,)
        sources = small[1:] + (target.at[pl.ds(goal_rows, depth)],)
        for j, (source, place) in enumerate(zip(sources, targets)):
            copies.append(pltpu.make_async_copy(source, place, sems.at[slots + 2 + j]))
    for copy in copies:
        copy.start()
    copies[0].wait()
    copies[1].wait()
    paired = [
        b_buf[pl.ds(pl.multiple_of(order[0, g] * size, size), size), :]
        for g in range(groups)
    ]
    high, low = split(cat(paired, 0))
    step = 2 if slots % 2 == 0 else 1
    for m in range(0, slots, step):
        for copy in copies[2 + m : 2 + m + step]:
            copy.wait()
        part = a_buf[m : m + step].reshape(step * depth, a_buf.shape[2])
        ah, al = split(part)
        both = mm(cat([ah, al], 0), high)
        both = both[: step * depth] + both[step * depth :] + mm(ah, low)
        out_ref[m : m + step] = both.reshape((step,) + out_ref.shape[1:])
    for copy in copies[2 + slots :]:
        copy.wait()
    if not own:
        once = jnp.where(group(1 - half) == 0, 1.0, 0.0)
        out_ref[0] -= goal[...] * once


def partial_product(order, top_rows, lower, slots, small=None):
    own = small is None
    depth, inner = top_rows.shape[0] // 2 // slots, top_rows.shape[1]
    out = jax.ShapeDtypeStruct((slots, depth, lower.shape[1]), F32)
    operands = (order, top_rows, lower) + (() if own else small)
    if not own:
        out = (out, jax.ShapeDtypeStruct((7,) + small[3].shape, F32))
    return pl.pallas_call(
        functools.partial(partial_kernel, own),
        out_shape=out,
        in_specs=[HBM] * len(operands),
        out_specs=VMEM if own else (VMEM, VMEM),
        scratch_shapes=[
            pltpu.SMEM(order.shape, jnp.int32),
            pltpu.VMEM((slots, depth, inner), F32),
            pltpu.VMEM(lower.shape, F32),
            pltpu.SemaphoreType.DMA((slots + 8,)),
            pltpu.VMEM((depth, lower.shape[1]), F32),
        ],
        compiler_params=params(),
        name="partial_own" if own else "partial_other",
    )(*operands)


def add_kernel(slots, a_ref, b_ref, *outs):
    for m in range(slots):
        outs[m][...] = a_ref[m] + b_ref[m]


def add_slots(a, b):
    slots = a.shape[0]
    shape = pltpu.VMEM(a.shape[1:], F32)
    return pl.pallas_call(
        functools.partial(add_kernel, slots),
        out_shape=(shape,) * slots,
        in_specs=[VMEM, VMEM],
        out_specs=(VMEM,) * slots,
        compiler_params=params(),
        name="add_slots",
    )(a, b)


def sum_kernel(*refs):
    total = refs[0][...]
    for r in refs[1:-1]:
        total = total + r[...]
    refs[-1][...] = total


def sum_slots(*parts):
    return pl.pallas_call(
        sum_kernel,
        out_shape=jax.ShapeDtypeStruct(parts[0].shape, F32),
        in_specs=[VMEM] * len(parts),
        out_specs=VMEM,
        compiler_params=params(),
        name="sum_slots",
    )(*parts)


def side_kernel(*refs):
    const, out = refs[-2:]
    total = refs[0][...]
    for r in refs[1:-2]:
        total = total + r[...]
    n = const.shape[1]
    for c in range(2):
        cols = slice(c * n, (c + 1) * n)
        out[:, cols] = block_dot(lhs(-total[:, cols]), block_rhs(const[c]))


def side_slot(parts, const):
    return pl.pallas_call(
        side_kernel,
        out_shape=jax.ShapeDtypeStruct(parts[0].shape, F32),
        in_specs=[VMEM] * (len(parts) + 1),
        out_specs=VMEM,
        compiler_params=params(),
        name="side_slot",
    )(*parts, const)


def first_block(k):
    return k * (k - 1) // 2


def prepare_kernel(u_hbm, q_hbm, p_hbm, const, out_ref, u_buf, q_buf, p_buf, sems):
    blocks, n, _ = p_buf.shape
    row = lax.axis_index("row")
    base = first_block(blocks)
    copies = [
        pltpu.make_async_copy(q_hbm, q_buf, sems.at[blocks]),
        pltpu.make_async_copy(p_hbm, p_buf, sems.at[blocks + 1]),
    ]
    for i in range(blocks - 1):
        first, count = (i + 1) * n, (blocks - 1 - i) * n
        cols = pl.multiple_of(row * (blocks * n) + first, n)
        copies.append(
            pltpu.make_async_copy(
                u_hbm.at[pl.ds(i * n, n), pl.ds(cols, count)],
                u_buf.at[pl.ds(i * n, n), pl.ds(first, count)],
                sems.at[i],
            )
        )
    for copy in copies:
        copy.start()
    left = lhs(const[2])
    out_ref[base + 2 * blocks] = block_dot(left, block_rhs(const[0]))
    both = block_dot(left, block_rhs(const[4]))
    out_ref[base + 2 * blocks + 1] = block_dot(lhs(both), block_rhs(const[1]))
    out_ref[base + 2 * blocks + 2] = block_dot(lhs(const[3]), block_rhs(const[1]))
    out_ref[base + 2 * blocks + 3, :blocks] = const[5, :blocks]
    for copy in copies[:2]:
        copy.wait()
    p = [block_rhs(p_buf[k]) for k in range(blocks)]
    out_ref[base + blocks : base + 2 * blocks] = p_buf[...]
    for i in range(blocks):
        q = lhs(q_buf[i])
        out_ref[base + i] = block_dot(q, p[i])
        if i + 1 == blocks:
            break
        copies[2 + i].wait()
        qu = wide_dot(q, wide_rhs(u_buf[i * n : (i + 1) * n, (i + 1) * n :]))
        for k in range(i + 1, blocks):
            own = qu[:, (k - i - 1) * n : (k - i) * n]
            out_ref[first_block(k) + i] = block_dot(lhs(own), p[k])


def prepare(corner, q, p, const):
    blocks, n, _ = q.shape
    count = first_block(blocks) + 2 * blocks + 4
    return pl.pallas_call(
        prepare_kernel,
        out_shape=pltpu.HBM((count, n, n), F32),
        in_specs=[HBM, HBM, HBM, VMEM],
        out_specs=VMEM,
        scratch_shapes=[
            pltpu.VMEM((blocks * n, blocks * n), F32),
            pltpu.VMEM(q.shape, F32),
            pltpu.VMEM(p.shape, F32),
            pltpu.SemaphoreType.DMA((blocks + 2,)),
        ],
        compiler_params=params(),
        name="prepare",
    )(corner, q, p, const)


def stage_kernel(count, u_hbm, t_ref, q_ref, *refs):
    sources, refs = refs[:count], refs[count:]
    targets, refs = refs[:count], refs[count:]
    near_ref, q_near_ref, out_ref, u_buf, sems = refs
    q_near_ref[...] = q_ref[...]
    blocks, half, wide = out_ref.shape
    n = wide // 2
    base = first_block(blocks) + blocks

    @pl.when(lax.axis_index("row") == 0)
    def _():
        columns = [
            pltpu.make_async_copy(
                u_hbm.at[:, pl.ds(half + k * n, n)], u_buf.at[k], sems.at[k]
            )
            for k in range(blocks)
        ]
        moves = [
            pltpu.make_async_copy(sources[j], targets[j], sems.at[blocks + j])
            for j in range(count)
        ]
        for copy in columns + moves:
            copy.start()
        for k in range(blocks):
            columns[k].wait()
            out_ref[k] = lhs(block_dot(lhs(u_buf[k]), block_rhs(t_ref[base + k])))
        near_ref[...] = t_ref[...]
        for copy in moves:
            copy.wait()

    @pl.when(lax.axis_index("row") != 0)
    def _():
        part = pl.ds(base, blocks)
        copy = pltpu.make_async_copy(sources[0].at[part], targets[0].at[part], sems.at[0])
        copy.start()
        copy.wait()


def stage(corner, shipped, q, *arrays):
    half = corner.shape[0]
    n = shipped.shape[1]
    blocks = half // n
    count = len(arrays)
    return pl.pallas_call(
        functools.partial(stage_kernel, count),
        out_shape=tuple(
            jax.ShapeDtypeStruct(a.shape, F32) for a in arrays + (shipped, q)
        )
        + (jax.ShapeDtypeStruct((blocks, half, 2 * n), BF16),),
        in_specs=[HBM, VMEM, VMEM] + [HBM] * count,
        out_specs=(VMEM,) * (3 + count),
        scratch_shapes=[
            pltpu.VMEM((blocks, half, n), F32),
            pltpu.SemaphoreType.DMA((blocks + count,)),
        ],
        compiler_params=params(),
        name="stage",
    )(corner, shipped, q, *arrays)


def chain_kernel(lower, *refs):
    if lower:
        parts, refs = refs[:-7], refs[-7:]
        q_ref, t_ref, const, z_ref, h_ref, c_buf, r_buf = refs
    else:
        c_ref, w_ref, t_ref, const, x_hbm, c_buf, x_buf, sems = refs
    row = lax.axis_index("row")
    n = t_ref.shape[1]
    blocks = c_buf.shape[0] // n
    base = first_block(blocks)
    left = slice(0, n)
    right = slice(n, 2 * n)

    def rows(i):
        return slice(i * n, (i + 1) * n)

    if lower:
        where = position(row, len(parts))
        for m, part in enumerate(parts):
            depth = part.shape[0]
            slot = where ^ mask_at(len(parts), row, m)
            first = pl.multiple_of(slot * depth, 8)
            r_buf[pl.ds(first, depth), :] = part[...]

        def rotated(i):
            return wide_dot(lhs(q_ref[i]), wide_rhs(r_buf[rows(i), :]))

    if not lower:
        nl = [block_rhs(const[2 + c]) for c in range(2)]
        copies = [
            pltpu.make_async_copy(
                x_buf.at[pl.ds(i * n, n)], x_hbm.at[pl.ds(i * n, n)], sems.at[i]
            )
            for i in range(blocks)
        ]

    def finish(i, y):
        x_buf[rows(i), :] = wide_dot(lhs(t_ref[base + blocks + i]), wide_rhs(y))
        copies[i].start()

    def columns(z0, z1):
        return cat([block_dot(lhs(z0), nl[0]), block_dot(lhs(z1), nl[1])], 1)

    @pl.when(row == 0)
    def _():
        bv = const[6, :8]
        g0, g01, g1 = (block_rhs(t_ref[base + 2 * blocks + j]) for j in range(3))
        av = t_ref[base + 2 * blocks + 3, : 8 * ((blocks + 7) // 8), :]

        def inverse(i, c):
            own = jnp.transpose(jnp.broadcast_to(av[i : i + 1, :], (n, n)))
            return 1.0 / (own + jnp.broadcast_to(bv[c : c + 1, :], (n, n)))

        def column(first, count, k):
            start = first_block(k) + first
            return lhs(t_ref[start : start + count].reshape(count * n, n))

        if lower:
            c_buf[rows(blocks - 1), :] = rotated(blocks - 1)
            c_buf[: (blocks - 1) * n, :] = jnp.zeros(((blocks - 1) * n, 2 * n), F32)
        else:
            c_buf[...] = c_ref[...] - w_ref[...]
        z0s, z1s = {}, {}
        for i in range(blocks - 1, -2, -1):
            if i >= 0:
                z0s[i] = c_buf[rows(i), left] * inverse(i, 0)
                z = lhs(z0s[i])
                h0f, j0 = block_dot(z, g0), block_dot(z, g01)
            if i + 1 < blocks and (lower or i >= 0):
                h1f = block_dot(lhs(z1s[i + 1]), g1)
                if lower:
                    z_ref[rows(i + 1), right] = z1s[i + 1]
                    h_ref[rows(i + 1), right] = h1f
            if lower and i > 0:
                c_buf[rows(i - 1), :] += rotated(i - 1)
            if not lower and i + 1 < blocks:
                y = columns(z0s[i + 1], z1s[i + 1])
            if i >= 0:
                h0 = block_rhs(h0f)
                if i > 0:
                    c_buf[rows(i - 1), left] -= block_dot(column(i - 1, 1, i), h0)
                coupled = block_dot(lhs(t_ref[base + i]), block_rhs(j0))
                c1 = c_buf[rows(i), right]
                if i + 1 < blocks:
                    h1 = block_rhs(h1f)
                    c1 = c1 - block_dot(column(i, 1, i + 1), h1)
                z1s[i] = (c1 - coupled) * inverse(i, 1)
                if lower:
                    z_ref[rows(i), left] = z0s[i]
                    h_ref[rows(i), left] = h0f
                if i > 1:
                    c_buf[: (i - 1) * n, left] -= block_dot(column(0, i - 1, i), h0)
                if i > 0 and i + 1 < blocks:
                    c_buf[: i * n, right] -= block_dot(column(0, i, i + 1), h1)
            if not lower and i + 1 < blocks:
                finish(i + 1, y)

    @pl.when(row != 0)
    def _():
        if lower:
            for i in range(blocks):
                z_ref[rows(i), :] = rotated(i)
        else:
            for i in range(blocks):
                finish(i, columns(c_ref[rows(i), left], c_ref[rows(i), right]))

    if not lower:
        for copy in copies:
            copy.wait()


def chain_lower(parts, q, t, const):
    blocks, n, _ = q.shape
    dims = (blocks * n, parts[0].shape[1])
    shape = jax.ShapeDtypeStruct(dims, F32)
    return pl.pallas_call(
        functools.partial(chain_kernel, True),
        out_shape=(shape, shape),
        in_specs=[VMEM] * (len(parts) + 3),
        out_specs=(VMEM, VMEM),
        scratch_shapes=[
            pltpu.VMEM(dims, F32),
            pltpu.VMEM(dims, F32),
        ],
        compiler_params=params(),
        name="chain_lower",
    )(*parts, q, t, const)


def chain_upper(c, w, t, const):
    blocks = c.shape[0] // t.shape[1]
    return pl.pallas_call(
        functools.partial(chain_kernel, False),
        out_shape=jax.ShapeDtypeStruct(c.shape, F32),
        in_specs=[VMEM] * 4,
        out_specs=HBM,
        scratch_shapes=[
            pltpu.VMEM(c.shape, F32),
            pltpu.VMEM(c.shape, F32),
            pltpu.SemaphoreType.DMA((blocks,)),
        ],
        compiler_params=params(),
        name="chain_upper",
    )(c, w, t, const)


def apply_kernel(u_ref, h_ref, q_ref, w_ref):
    blocks, _, wide = u_ref.shape
    n = wide // 2

    @pl.when(lax.axis_index("row") == 0)
    def _():
        total = None
        for k in range(blocks):
            term = wide_dot(u_ref[k], wide_rhs(h_ref[k * n : (k + 1) * n, :]))
            total = term if total is None else total + term
        for i in range(blocks):
            rows = slice(i * n, (i + 1) * n)
            w_ref[rows, :] = wide_dot(lhs(q_ref[i]), wide_rhs(total[rows, :]))


def apply_cross(cross, h, q):
    return pl.pallas_call(
        apply_kernel,
        out_shape=jax.ShapeDtypeStruct(h.shape, F32),
        in_specs=[VMEM] * 3,
        out_specs=VMEM,
        compiler_params=params(),
        name="apply_cross",
    )(cross, h, q)


def exchange(block, masks):
    count = len(masks)
    route = [
        (i * count + r, (i ^ masks[r]) * count + r)
        for i in range(lax.axis_size("col"))
        for r in range(count)
    ]
    return lax.ppermute(block, ("col", "row"), route)


def exchange_at(block, slots, k):
    cols = lax.axis_size("col")
    return exchange(
        block, [device_mask(cols, r, masks[k]) for r, masks in enumerate(orders(slots))]
    )


def swap_rows(block):
    return lax.ppermute(block, "row", [(0, 1), (1, 0)])


def far(x):
    return pltpu.with_memory_space_constraint(x, pltpu.HBM)


def body(
    top_rows, lower_new, block_order, corner, target, coupling,
    top_right, top_left, top_values, new_right, new_left, new_values,
):
    cols = lax.axis_size("col")
    slots = min(cols, 8)
    small = (target, new_right, new_left, coupling, top_values, new_values)
    small = tuple(map(far, small))
    block_order, top_rows, lower_new, corner, top_left, top_right = map(
        far, (block_order, top_rows, lower_new, corner, top_left, top_right)
    )

    theirs, const = partial_product(block_order, top_rows, lower_new, slots, small)
    theirs = swap_rows(theirs)
    ours = partial_product(block_order, top_rows, lower_new, slots)
    q_other = swap_rows(top_left)
    pieces = add_slots(ours, theirs)
    received = [exchange_at(pieces[m], slots, m) for m in range(1, slots)]
    packed = prepare(corner, top_left, top_right, const)
    shipped = swap_rows(packed)
    packed_near, q_own, near, q_near, cross = stage(
        corner, shipped, q_other, far(packed), top_left
    )

    total = sum_slots(pieces[0], *received)
    last = []
    finals = list(zip(last_masks(cols, 0), last_masks(cols, 1)))
    for step, masks in enumerate(finals):
        moved = exchange(total, masks)
        if step + 1 < len(finals):
            total = total + moved
        else:
            last = [moved]
    side = side_slot([total] + last, const)
    parts = [side] + [exchange_at(side, slots, m) for m in range(1, slots)]
    z_lower, h = chain_lower(parts, q_near, near, const)
    moved = swap_rows(z_lower)
    w = apply_cross(cross, h, q_own)
    return chain_upper(moved, w, packed_near, const)


def solution(mesh):
    placed = (
        P(None, ("col", "row")),
        P(("col", "row"), None),
        P(("col", "row"), None),
        P("row", None),
        P("row", None),
        P(),
        P("row", None, None),
        P("row", None, None),
        P("row", None),
        P(),
        P(),
        P(),
    )
    return jax.shard_map(
        body, mesh=mesh, in_specs=placed, out_specs=P("row", None), check_vma=False
    )
```

```python
import functools
import math

import jax
import jax.numpy as jnp
from jax import lax
from jax.experimental import pallas as pl
from jax.experimental.pallas import tpu as pltpu
from jax.sharding import PartitionSpec as P


F32 = jnp.float32
BF16 = jnp.bfloat16
GRANT = 12 << 20

VMEM = pl.BlockSpec(memory_space=pltpu.VMEM)
ANY = pl.BlockSpec(memory_space=pl.ANY)
HBM = pl.BlockSpec(memory_space=pltpu.HBM)


def split(x):
    high = x.astype(BF16)
    return high, (x - high.astype(F32)).astype(BF16)


def mm(a, b):
    return jnp.dot(a, b, preferred_element_type=F32)


def cat(parts, axis):
    return jnp.concatenate(parts, axis=axis)


def lhs(x):
    return cat(split(x), 1)


def wide_rhs(x):
    high, low = split(x)
    return cat([high, high], 0), low


def wide_dot(a, b):
    n = a.shape[1] // 2
    return mm(a, b[0]) + mm(a[:, :n], b[1])


def block_rhs(x):
    both = cat(split(x), 1)
    return cat([both, both], 0)


def block_dot(a, b):
    n = b.shape[1] // 2
    r = mm(a, b)
    return r[:, :n] + r[:, n:]


def params(**kw):
    return pltpu.CompilerParams(vmem_limit_bytes=GRANT, **kw)


def orders(slots, gather=False):
    if gather:
        rows = ((0, 6, 1, 7, 3, 5, 4, 2), (0, 7, 6, 5, 4, 3, 1, 2))
    else:
        rows = ((0, 7, 3, 5, 6, 4, 1, 2), (0, 1, 2, 3, 4, 5, 6, 7))
    return tuple(tuple(m for m in masks if m < slots) for masks in rows)


def mask_at(slots, row, k, gather=False):
    first, second = (masks[k] for masks in orders(slots, gather))
    return first + row * (second - first)


def device_mask(cols, row, mask):
    if row == 1 and cols >= 16 and mask & 4:
        return (mask & 3) | 12
    return mask


def last_masks(cols, row):
    slots = min(cols, 8)
    masks = [slots << k for k in range((cols // slots).bit_length() - 1)]
    if row == 1 and cols >= 16:
        masks[0] = 4
    return masks


def position(row, slots):
    col = lax.axis_index("col")
    first = col & (slots - 1)
    if lax.axis_size("col") < 16:
        return first
    second = (col & 3) | (((col >> 3) & 1) << 2)
    return first + row * (second - first)


def group(row):
    col = lax.axis_index("col")
    if lax.axis_size("col") < 16:
        return col & 0
    second = ((col >> 4) << 1) | (((col >> 2) ^ (col >> 3)) & 1)
    first = col >> 3
    return first + row * (second - first)


def partial_kernel(own, order_hbm, a_hbm, b_hbm, *refs):
    small, refs = (refs[:6], refs[6:]) if not own else ((), refs)
    out_ref, refs = refs[0], refs[1:]
    const_ref, refs = (refs[0], refs[1:]) if not own else (None, refs)
    order, a_buf, b_buf, sems, goal = refs
    slots, depth, _ = out_ref.shape
    groups = order.shape[1]
    size = b_buf.shape[0] // groups
    row = lax.axis_index("row")
    half = 1 - row if own else row
    where = position(1 - half, slots)
    copies = [
        pltpu.make_async_copy(order_hbm, order, sems.at[slots]),
        pltpu.make_async_copy(b_hbm, b_buf, sems.at[slots + 1]),
    ]
    for m in range(slots):
        slot = where ^ mask_at(slots, 1 - half, m)
        rows = pl.multiple_of((half * slots + slot) * depth, 8)
        copies.append(
            pltpu.make_async_copy(a_hbm.at[pl.ds(rows, depth)], a_buf.at[m], sems.at[m])
        )
    if not own:
        target, _, _, _, av, bv = small
        goal_rows = pl.multiple_of(where * depth, 8)
        targets = (
            const_ref.at[pl.ds(0, 2)],
            const_ref.at[pl.ds(2, 2)],
            const_ref.at[4],
            const_ref.at[5, pl.ds(0, av.shape[0])],
            const_ref.at[6, pl.ds(0, bv.shape[0])],
        )
        targets += (goal,)
        sources = small[1:] + (target.at[pl.ds(goal_rows, depth)],)
        for j, (source, place) in enumerate(zip(sources, targets)):
            copies.append(pltpu.make_async_copy(source, place, sems.at[slots + 2 + j]))
    for copy in copies:
        copy.start()
    copies[0].wait()
    copies[1].wait()
    paired = [
        b_buf[pl.ds(pl.multiple_of(order[0, g] * size, size), size), :]
        for g in range(groups)
    ]
    high, low = split(cat(paired, 0))
    step = math.gcd(slots, 4)
    for m in range(0, slots, step):
        for copy in copies[2 + m : 2 + m + step]:
            copy.wait()
        part = a_buf[m : m + step].reshape(step * depth, a_buf.shape[2])
        ah, al = split(part)
        both = mm(cat([ah, al], 0), high)
        both = both[: step * depth] + both[step * depth :] + mm(ah, low)
        out_ref[m : m + step] = both.reshape((step,) + out_ref.shape[1:])
    for copy in copies[2 + slots :]:
        copy.wait()
    if not own:
        once = jnp.where(group(1 - half) == 0, 1.0, 0.0)
        out_ref[0] -= goal[...] * once


def partial_product(order, top_rows, lower, slots, small=None):
    own = small is None
    depth, inner = top_rows.shape[0] // 2 // slots, top_rows.shape[1]
    out = jax.ShapeDtypeStruct((slots, depth, lower.shape[1]), F32)
    operands = (order, top_rows, lower) + (() if own else small)
    if not own:
        out = (out, jax.ShapeDtypeStruct((7,) + small[3].shape, F32))
    return pl.pallas_call(
        functools.partial(partial_kernel, own),
        out_shape=out,
        in_specs=[HBM] * len(operands),
        out_specs=VMEM if own else (VMEM, VMEM),
        scratch_shapes=[
            pltpu.SMEM(order.shape, jnp.int32),
            pltpu.VMEM((slots, depth, inner), F32),
            pltpu.VMEM(lower.shape, F32),
            pltpu.SemaphoreType.DMA((slots + 8,)),
            pltpu.VMEM((depth, lower.shape[1]), F32),
        ],
        compiler_params=params(),
        name="partial_own" if own else "partial_other",
    )(*operands)


def add_kernel(slots, a_ref, b_ref, *outs):
    for m in range(slots):
        outs[m][...] = a_ref[m] + b_ref[m]


def add_slots(a, b):
    slots = a.shape[0]
    shape = pltpu.VMEM(a.shape[1:], F32)
    return pl.pallas_call(
        functools.partial(add_kernel, slots),
        out_shape=(shape,) * slots,
        in_specs=[VMEM, VMEM],
        out_specs=(VMEM,) * slots,
        compiler_params=params(),
        name="add_slots",
    )(a, b)


def sum_kernel(*refs):
    total = refs[0][...]
    for r in refs[1:-1]:
        total = total + r[...]
    refs[-1][...] = total


def sum_slots(*parts):
    return pl.pallas_call(
        sum_kernel,
        out_shape=jax.ShapeDtypeStruct(parts[0].shape, F32),
        in_specs=[VMEM] * len(parts),
        out_specs=VMEM,
        compiler_params=params(),
        name="sum_slots",
    )(*parts)


def side_kernel(*refs):
    const, out = refs[-2:]
    total = refs[0][...]
    for r in refs[1:-2]:
        total = total + r[...]
    n = const.shape[1]
    for c in range(2):
        cols = slice(c * n, (c + 1) * n)
        out[:, cols] = block_dot(lhs(-total[:, cols]), block_rhs(const[c]))


def side_slot(parts, const):
    return pl.pallas_call(
        side_kernel,
        out_shape=jax.ShapeDtypeStruct(parts[0].shape, F32),
        in_specs=[VMEM] * (len(parts) + 1),
        out_specs=VMEM,
        compiler_params=params(),
        name="side_slot",
    )(*parts, const)


def first_block(k):
    return k * (k - 1) // 2


def prepare_kernel(
    u_hbm, q_hbm, p_hbm, const, out_hbm, out_ref, u_buf, q_buf, p_buf, sems, out_sems
):
    blocks, n, _ = p_buf.shape
    row = lax.axis_index("row")
    written = []

    def write(first, count):
        part = pl.ds(first, count)
        copy = pltpu.make_async_copy(
            out_ref.at[part], out_hbm.at[part], out_sems.at[len(written)]
        )
        copy.start()
        written.append(copy)

    base = first_block(blocks)
    copies = [
        pltpu.make_async_copy(q_hbm, q_buf, sems.at[blocks]),
        pltpu.make_async_copy(p_hbm, p_buf, sems.at[blocks + 1]),
    ]
    for i in range(blocks - 1):
        first, count = (i + 1) * n, (blocks - 1 - i) * n
        cols = pl.multiple_of(row * (blocks * n) + first, n)
        copies.append(
            pltpu.make_async_copy(
                u_hbm.at[pl.ds(i * n, n), pl.ds(cols, count)],
                u_buf.at[pl.ds(i * n, n), pl.ds(first, count)],
                sems.at[i],
            )
        )
    for copy in copies:
        copy.start()
    left = lhs(const[2])
    out_ref[base + 2 * blocks] = block_dot(left, block_rhs(const[0]))
    both = block_dot(left, block_rhs(const[4]))
    out_ref[base + 2 * blocks + 1] = block_dot(lhs(both), block_rhs(const[1]))
    out_ref[base + 2 * blocks + 2] = block_dot(lhs(const[3]), block_rhs(const[1]))
    out_ref[base + 2 * blocks + 3, :blocks] = const[5, :blocks]
    for copy in copies[:2]:
        copy.wait()
    p = [block_rhs(p_buf[k]) for k in range(blocks)]
    out_ref[base + blocks : base + 2 * blocks] = p_buf[...]
    write(base + blocks, blocks + 4)
    for i in range(blocks):
        q = lhs(q_buf[i])
        out_ref[base + i] = block_dot(q, p[i])
    write(base, blocks)
    for i in range(blocks - 1):
        q = lhs(q_buf[i])
        copies[2 + i].wait()
        qu = wide_dot(q, wide_rhs(u_buf[i * n : (i + 1) * n, (i + 1) * n :]))
        for k in range(i + 1, blocks):
            own = qu[:, (k - i - 1) * n : (k - i) * n]
            out_ref[first_block(k) + i] = block_dot(lhs(own), p[k])
        write(first_block(i + 1), i + 1)
    for copy in written:
        copy.wait()


def prepare(corner, q, p, const):
    blocks, n, _ = q.shape
    count = first_block(blocks) + 2 * blocks + 4
    return pl.pallas_call(
        prepare_kernel,
        out_shape=pltpu.HBM((count, n, n), F32),
        in_specs=[HBM, HBM, HBM, VMEM],
        out_specs=HBM,
        scratch_shapes=[
            pltpu.VMEM((count, n, n), F32),
            pltpu.VMEM((blocks * n, blocks * n), F32),
            pltpu.VMEM(q.shape, F32),
            pltpu.VMEM(p.shape, F32),
            pltpu.SemaphoreType.DMA((blocks + 2,)),
            pltpu.SemaphoreType.DMA((blocks + 1,)),
        ],
        compiler_params=params(),
        name="prepare",
    )(corner, q, p, const)


def stage_kernel(count, u_hbm, t_ref, q_any, *refs):
    sources, refs = refs[:count], refs[count:]
    targets, refs = refs[:count], refs[count:]
    q_near_ref, out_ref, u_buf, sems = refs
    q_copy = pltpu.make_async_copy(q_any, q_near_ref, sems.at[q_any.shape[0] + count])
    q_copy.start()
    blocks, half, wide = out_ref.shape
    n = wide // 2
    base = first_block(blocks) + blocks

    @pl.when(lax.axis_index("row") == 0)
    def _():
        columns = [
            pltpu.make_async_copy(
                u_hbm.at[:, pl.ds(half + k * n, n)], u_buf.at[k], sems.at[k]
            )
            for k in range(blocks)
        ]
        moves = [
            pltpu.make_async_copy(sources[j], targets[j], sems.at[blocks + j])
            for j in range(count)
        ]
        for copy in columns + moves:
            copy.start()
        for k in range(blocks):
            columns[k].wait()
            out_ref[k] = lhs(block_dot(lhs(u_buf[k]), block_rhs(t_ref[base + k])))
        for copy in moves:
            copy.wait()

    @pl.when(lax.axis_index("row") != 0)
    def _():
        part = pl.ds(base, blocks)
        copy = pltpu.make_async_copy(sources[0].at[part], targets[0].at[part], sems.at[0])
        copy.start()
        copy.wait()

    q_copy.wait()


def stage(corner, shipped, q, *arrays):
    half = corner.shape[0]
    n = shipped.shape[1]
    blocks = half // n
    count = len(arrays)
    return pl.pallas_call(
        functools.partial(stage_kernel, count),
        out_shape=tuple(
            jax.ShapeDtypeStruct(a.shape, F32) for a in arrays + (q,)
        )
        + (jax.ShapeDtypeStruct((blocks, half, 2 * n), BF16),),
        in_specs=[HBM, VMEM, ANY] + [HBM] * count,
        out_specs=(VMEM,) * (2 + count),
        scratch_shapes=[
            pltpu.VMEM((blocks, half, n), F32),
            pltpu.SemaphoreType.DMA((blocks + count + 1,)),
        ],
        compiler_params=params(),
        name="stage",
    )(corner, shipped, q, *arrays)


def chain_kernel(lower, *refs):
    if lower:
        parts, refs = refs[:-7], refs[-7:]
        q_ref, t_ref, const, z_ref, h_ref, c_buf, r_buf = refs
    else:
        c_ref, w_ref, t_ref, const, x_hbm, c_buf, x_buf, sems = refs
    row = lax.axis_index("row")
    n = t_ref.shape[1]
    blocks = c_buf.shape[0] // n
    base = first_block(blocks)
    left = slice(0, n)
    right = slice(n, 2 * n)

    def rows(i):
        return slice(i * n, (i + 1) * n)

    if lower:
        where = position(row, len(parts))
        for m, part in enumerate(parts):
            depth = part.shape[0]
            slot = where ^ mask_at(len(parts), row, m, True)
            first = pl.multiple_of(slot * depth, 8)
            r_buf[pl.ds(first, depth), :] = part[...]

        def rotated(i):
            return wide_dot(lhs(q_ref[i]), wide_rhs(r_buf[rows(i), :]))

    if not lower:
        nl = [block_rhs(const[2 + c]) for c in range(2)]
        copies = [
            pltpu.make_async_copy(
                x_buf.at[pl.ds(i * n, n)], x_hbm.at[pl.ds(i * n, n)], sems.at[i]
            )
            for i in range(blocks)
        ]

    def finish(i, y):
        x_buf[rows(i), :] = wide_dot(lhs(t_ref[base + blocks + i]), wide_rhs(y))
        copies[i].start()

    def columns(z0, z1):
        return cat([block_dot(lhs(z0), nl[0]), block_dot(lhs(z1), nl[1])], 1)

    @pl.when(row == 0)
    def _():
        bv = const[6, :8]
        g0, g01, g1 = (block_rhs(t_ref[base + 2 * blocks + j]) for j in range(3))
        av = t_ref[base + 2 * blocks + 3, : 8 * ((blocks + 7) // 8), :]

        def inverse(i, c):
            own = jnp.transpose(jnp.broadcast_to(av[i : i + 1, :], (n, n)))
            return 1.0 / (own + jnp.broadcast_to(bv[c : c + 1, :], (n, n)))

        def column(first, count, k):
            start = first_block(k) + first
            return lhs(t_ref[start : start + count].reshape(count * n, n))

        if lower:
            c_buf[rows(blocks - 1), :] = rotated(blocks - 1)
            c_buf[: (blocks - 1) * n, :] = jnp.zeros(((blocks - 1) * n, 2 * n), F32)
        else:
            c_buf[...] = c_ref[...] - w_ref[...]
        z0s, z1s = {}, {}
        for i in range(blocks - 1, -2, -1):
            if i >= 0:
                z0s[i] = c_buf[rows(i), left] * inverse(i, 0)
                z = lhs(z0s[i])
                h0f, j0 = block_dot(z, g0), block_dot(z, g01)
            if i + 1 < blocks and (lower or i >= 0):
                h1f = block_dot(lhs(z1s[i + 1]), g1)
                if lower:
                    z_ref[rows(i + 1), right] = z1s[i + 1]
                    h_ref[rows(i + 1), right] = h1f
            if lower and i > 0:
                c_buf[rows(i - 1), :] += rotated(i - 1)
            if not lower and i + 1 < blocks:
                y = columns(z0s[i + 1], z1s[i + 1])
            if i >= 0:
                h0 = block_rhs(h0f)
                if i > 0:
                    c_buf[rows(i - 1), left] -= block_dot(column(i - 1, 1, i), h0)
                coupled = block_dot(lhs(t_ref[base + i]), block_rhs(j0))
                c1 = c_buf[rows(i), right]
                if i + 1 < blocks:
                    h1 = block_rhs(h1f)
                    c1 = c1 - block_dot(column(i, 1, i + 1), h1)
                z1s[i] = (c1 - coupled) * inverse(i, 1)
                if lower:
                    z_ref[rows(i), left] = z0s[i]
                    h_ref[rows(i), left] = h0f
                if i > 1:
                    c_buf[: (i - 1) * n, left] -= block_dot(column(0, i - 1, i), h0)
                if i > 0 and i + 1 < blocks:
                    c_buf[: i * n, right] -= block_dot(column(0, i, i + 1), h1)
            if not lower and i + 1 < blocks:
                finish(i + 1, y)

    @pl.when(row != 0)
    def _():
        if lower:
            for i in range(blocks):
                z_ref[rows(i), :] = rotated(i)
        else:
            for i in range(blocks):
                finish(i, columns(c_ref[rows(i), left], c_ref[rows(i), right]))

    if not lower:
        for copy in copies:
            copy.wait()


def chain_lower(parts, q, t, const):
    blocks, n, _ = q.shape
    dims = (blocks * n, parts[0].shape[1])
    shape = jax.ShapeDtypeStruct(dims, F32)
    return pl.pallas_call(
        functools.partial(chain_kernel, True),
        out_shape=(shape, shape),
        in_specs=[VMEM] * (len(parts) + 3),
        out_specs=(VMEM, VMEM),
        scratch_shapes=[
            pltpu.VMEM(dims, F32),
            pltpu.VMEM(dims, F32),
        ],
        compiler_params=params(),
        name="chain_lower",
    )(*parts, q, t, const)


def chain_upper(c, w, t, const):
    blocks = c.shape[0] // t.shape[1]
    return pl.pallas_call(
        functools.partial(chain_kernel, False),
        out_shape=jax.ShapeDtypeStruct(c.shape, F32),
        in_specs=[VMEM] * 4,
        out_specs=HBM,
        scratch_shapes=[
            pltpu.VMEM(c.shape, F32),
            pltpu.VMEM(c.shape, F32),
            pltpu.SemaphoreType.DMA((blocks,)),
        ],
        compiler_params=params(),
        name="chain_upper",
    )(c, w, t, const)


def apply_kernel(u_ref, h_ref, q_ref, w_ref):
    blocks, _, wide = u_ref.shape
    n = wide // 2

    @pl.when(lax.axis_index("row") == 0)
    def _():
        total = None
        for k in range(blocks):
            term = wide_dot(u_ref[k], wide_rhs(h_ref[k * n : (k + 1) * n, :]))
            total = term if total is None else total + term
        for i in range(blocks):
            rows = slice(i * n, (i + 1) * n)
            w_ref[rows, :] = wide_dot(lhs(q_ref[i]), wide_rhs(total[rows, :]))


def apply_cross(cross, h, q):
    return pl.pallas_call(
        apply_kernel,
        out_shape=jax.ShapeDtypeStruct(h.shape, F32),
        in_specs=[VMEM] * 3,
        out_specs=VMEM,
        compiler_params=params(),
        name="apply_cross",
    )(cross, h, q)


def exchange(block, masks):
    count = len(masks)
    route = [
        (i * count + r, (i ^ masks[r]) * count + r)
        for i in range(lax.axis_size("col"))
        for r in range(count)
    ]
    return lax.ppermute(block, ("col", "row"), route)


def exchange_at(block, slots, k, gather=False):
    cols = lax.axis_size("col")
    rows = orders(slots, gather)
    return exchange(
        block, [device_mask(cols, r, masks[k]) for r, masks in enumerate(rows)]
    )


def swap_rows(block):
    return lax.ppermute(block, "row", [(0, 1), (1, 0)])


def far(x):
    return pltpu.with_memory_space_constraint(x, pltpu.HBM)


def body(
    top_rows, lower_new, block_order, corner, target, coupling,
    top_right, top_left, top_values, new_right, new_left, new_values,
):
    cols = lax.axis_size("col")
    slots = min(cols, 8)
    small = (target, new_right, new_left, coupling, top_values, new_values)
    small = tuple(map(far, small))
    block_order, top_rows, lower_new, corner, top_left, top_right = map(
        far, (block_order, top_rows, lower_new, corner, top_left, top_right)
    )

    theirs, const = partial_product(block_order, top_rows, lower_new, slots, small)
    theirs = swap_rows(theirs)
    ours = partial_product(block_order, top_rows, lower_new, slots)
    q_other = swap_rows(top_left)
    pieces = add_slots(ours, theirs)
    received = [exchange_at(pieces[m], slots, m) for m in range(1, slots)]
    packed = prepare(corner, top_left, top_right, const)
    shipped = swap_rows(packed)
    packed_near, q_own, q_near, cross = stage(
        corner, shipped, q_other, far(packed), top_left
    )

    total = sum_slots(pieces[0], *received)
    last = []
    finals = list(zip(last_masks(cols, 0), last_masks(cols, 1)))
    for step, masks in enumerate(finals):
        moved = exchange(total, masks)
        if step + 1 < len(finals):
            total = total + moved
        else:
            last = [moved]
    side = side_slot([total] + last, const)
    parts = [side] + [exchange_at(side, slots, m, True) for m in range(1, slots)]
    z_lower, h = chain_lower(parts, q_near, shipped, const)
    moved = swap_rows(z_lower)
    w = apply_cross(cross, h, q_own)
    return chain_upper(moved, w, packed_near, const)


def solution(mesh):
    placed = (
        P(None, ("col", "row")),
        P(("col", "row"), None),
        P(("col", "row"), None),
        P("row", None),
        P("row", None),
        P(),
        P("row", None, None),
        P("row", None, None),
        P("row", None),
        P(),
        P(),
        P(),
    )
    return jax.shard_map(
        body, mesh=mesh, in_specs=placed, out_specs=P("row", None), check_vma=False
    )
```
